32 devices in a mesh: band: 8 (over y, x, core), samp: 4 (over z).
Axes of the slice: x: 2, y: 2, z: 4, core: 2. Of those that a mesh axis runs over, the one named last changes fastest.
Arguments:
- dosage: bfloat16 [8192, 4096], P('samp', 'band'), may hold values from -1 to 2, as said below
Outputs:
- linkage: float32 [4096, 2048], P(('band', 'samp'))
The draws below stay inside these ranges and needn't reach their ends.
Inputs may be any that keep to these rules, and one draw needn't show every extreme that they name: -1 marks a missing call; every other entry is an imputed dosage between 0 and 2.
All inputs are finite; a program needn't handle non-finite values.
Results may differ from the reference program's by a relative error of at most 0.0015.
Values may be sent and summed in bfloat16 or wider, within the bound.
A program may use at most 64 MiB of HBM per device.

```python
import jax
import jax.numpy as jnp
from jax import lax

TILE = 512
WIN = 2048
SAMPLES = 8192
SNPS = 4096


def draw_dosage(key, part):
    keys = jax.random.split(jax.random.fold_in(key, 17), 6)
    position = jnp.arange(SAMPLES, dtype=jnp.float32) / SAMPLES
    cohort = 0.5 + 1.5 * position
    freq = jax.random.uniform(keys[0], (SNPS,), jnp.float32, 0.05, 0.5)
    noise = 0.25 * jax.random.normal(keys[2], (SAMPLES, SNPS), jnp.float32)
    chance = jnp.clip(freq[None, :] * cohort[:, None], 0.0, 0.95)
    first = (jax.random.uniform(keys[1], (SAMPLES, SNPS), jnp.float32) < chance).astype(jnp.float32)
    second = (jax.random.uniform(keys[5], (SAMPLES, SNPS), jnp.float32) < chance).astype(jnp.float32)
    dose = jnp.clip(first + second + noise, 0.0, 2.0)
    rate = 0.02 + 0.1 * position
    missing = jax.random.uniform(keys[3], (SAMPLES, SNPS), jnp.float32) < rate[:, None]
    return jnp.where(missing, -1.0, dose).astype(jnp.bfloat16)


def setup_inputs(seed: int = 0) -> dict:
    key_of = jax.random.split(jax.random.key(seed), 2)
    return {
        "dosage": draw_dosage(jax.random.fold_in(key_of[1], 71), 0),
    }


def reference(dosage):
    raw = dosage.astype(jnp.float32)
    observed = (raw >= 0.0).astype(jnp.float32)
    values = observed * raw
    count = lax.optimization_barrier(jnp.sum(observed, axis=0))
    total = lax.optimization_barrier(jnp.sum(values, axis=0))
    square = lax.optimization_barrier(jnp.sum(values * values, axis=0))
    mean = (total + 1.0) / (count + 1.0)
    spread = (square - 2.0 * mean * total + count * mean * mean + 0.5) / (count + 1.0)
    scaled = (observed * (values - mean) * lax.rsqrt(spread)).astype(jnp.bfloat16)
    padded = jnp.pad(scaled, ((0, 0), (0, WIN - TILE)))

    def one_tile(index):
        rows = lax.dynamic_slice_in_dim(scaled, index * TILE, TILE, 1)
        columns = lax.dynamic_slice_in_dim(padded, index * TILE, WIN, 1)
        product = lax.dot_general(rows, columns, (((0,), (0,)), ((), ())), preferred_element_type=jnp.float32)
        return product / SAMPLES
    blocks = lax.map(one_tile, jnp.arange(SNPS // TILE, dtype=jnp.int32))
    return blocks.reshape(SNPS, WIN)
```

```python
import functools

import jax
import jax.numpy as jnp
from jax import lax
from jax.experimental import pallas as pl
from jax.experimental.pallas import tpu as pltpu
from jax.sharding import PartitionSpec as P

TILE = 512
WIN = 2048
PIECES = 2
WIRE = jnp.float32
MESH = pl.DeviceIdType.MESH


def remote(src, dst, send, recv, band, samp):
    return pltpu.make_async_remote_copy(
        src_ref=src, dst_ref=dst, send_sem=send, recv_sem=recv,
        device_id=(band, samp), device_id_type=MESH,
    )


def kernel(bands, shards, reach, samples, raw_ref, out_ref, own_t, window, stats, stats_in, coef,
           coef_in, total_ref, parts, parts_in, panel_s, panel_r, stat_s, stat_r, coef_s, coef_r,
           part_s, part_r):
    band = lax.axis_index("band")
    samp = lax.axis_index("samp")
    depth, width = raw_ref.shape
    rows = width // shards
    piece = width // PIECES
    peers = [lax.rem(samp + d, shards) for d in range(1, shards)]

    barrier = pltpu.get_barrier_semaphore()
    for peer in peers:
        pl.semaphore_signal(barrier, inc=1, device_id=(band, peer), device_id_type=MESH)
    expected = shards - 1
    for k in range(1, reach + 1):
        @pl.when(band >= k)
        def _():
            pl.semaphore_signal(barrier, inc=1, device_id=(band - k, samp), device_id_type=MESH)

        @pl.when(band + k < bands)
        def _():
            pl.semaphore_signal(barrier, inc=1, device_id=(band + k, samp), device_id_type=MESH)
    expected = expected + jnp.minimum(band, reach) + jnp.minimum(bands - 1 - band, reach)
    pl.semaphore_wait(barrier, expected)

    def panel_copy(k, j):
        columns = pl.ds(j * piece, piece)
        return remote(raw_ref.at[:, columns], window.at[k - 1, :, columns],
                      panel_s.at[k - 1, j], panel_r.at[k - 1, j], jnp.maximum(band - k, 0), samp)

    def coef_copy(k):
        return remote(coef, coef_in.at[k - 1], coef_s.at[k - 1], coef_r.at[k - 1],
                      jnp.maximum(band - k, 0), samp)

    def part_copy(k, j, d):
        columns = pl.ds(k * width + j * piece, piece)
        return remote(parts.at[pl.ds(pl.multiple_of(peers[d] * rows, rows), rows), columns],
                      parts_in.at[d, :, columns],
                      part_s.at[k, j, d], part_r.at[k, j, d], band, peers[d])

    def start_panel(k, j):
        @pl.when(band >= k)
        def _():
            panel_copy(k, j).start()

    early = [(k, 0) for k in range(1, min(reach, 2) + 1)]
    later = [(k, j) for j in range(PIECES) for k in range(1, reach + 1) if (k, j) not in early]
    for k, j in early:
        start_panel(k, j)

    step = 64

    def add(i, carry):
        x = raw_ref[pl.ds(pl.multiple_of(i * step, step), step), :].astype(jnp.float32)
        seen = jnp.where(x >= 0.0, 1.0, 0.0)
        value = jnp.where(x >= 0.0, x, 0.0)
        fold = lambda a: jnp.sum(a.reshape(step // 8, 8, width), axis=0)
        return carry[0] + fold(seen), carry[1] + fold(value), carry[2] + fold(value * value)

    zero = jnp.zeros((8, width), jnp.float32)
    sums = lax.fori_loop(0, depth // step, add, (zero, zero, zero))
    stats[...] = jnp.concatenate(
        [jnp.sum(a, axis=0, keepdims=True) for a in sums] + [jnp.zeros((5, width), jnp.float32)], axis=0
    )
    stat_copies = [
        remote(stats, stats_in.at[d], stat_s.at[d], stat_r.at[d], band, peers[d])
        for d in range(shards - 1)
    ]
    for copy in stat_copies:
        copy.start()
    for copy in stat_copies:
        copy.wait()
    sums = stats[...]
    for d in range(shards - 1):
        sums = sums + stats_in[d]
    count, total, square = sums[0:1], sums[1:2], sums[2:3]
    mean = (total + 1.0) / (count + 1.0)
    spread = (square - 2.0 * mean * total + count * mean * mean + 0.5) / (count + 1.0)
    coef[...] = jnp.concatenate(
        [mean, lax.rsqrt(spread), jnp.zeros((6, width), jnp.float32)], axis=0
    )
    for k in range(1, reach + 1):
        @pl.when(band >= k)
        def _():
            coef_copy(k).start()
    for k, j in later:
        start_panel(k, j)

    chunk = 256

    def standard(x, mean, scale):
        x = x.astype(jnp.float32)
        return jnp.where(x >= 0.0, (x - mean) * scale, 0.0).astype(jnp.bfloat16)

    own = window.at[reach]

    def scale_own(i, _):
        span = pl.ds(pl.multiple_of(i * chunk, chunk), chunk)
        scaled = standard(raw_ref[span, :], coef[0:1, :], coef[1:2, :])
        own[span, :] = scaled
        own_t[:, span] = scaled.T
        return 0

    lax.fori_loop(0, depth // chunk, scale_own, 0)

    def correlate(k, j, panel):
        columns = slice(j * piece, (j + 1) * piece)
        place = slice(k * width + j * piece, k * width + (j + 1) * piece)

        def block(i, _):
            span = pl.ds(pl.multiple_of(i * 256, 256), 256)
            total_ref[span, :] = jnp.dot(
                own_t[span, :], panel[:, columns], preferred_element_type=jnp.float32
            )
            parts[span, place] = total_ref[span, :].astype(WIRE)
            return 0

        lax.fori_loop(0, width // 256, block, 0)
        for d in range(shards - 1):
            part_copy(k, j, d).start()
        out_ref[:, place] = total_ref[pl.ds(pl.multiple_of(samp * rows, rows), rows), :]

    def finish(k, j):
        place = slice(k * width + j * piece, k * width + (j + 1) * piece)
        total = out_ref[:, place]
        for d in range(shards - 1):
            part_copy(k, j, d).wait()
            total = total + parts_in[d, :, place].astype(jnp.float32)
        out_ref[:, place] = total / samples

    for j in range(PIECES):
        correlate(0, j, own)
    for j in range(PIECES):
        for k in range(1, reach + 1):
            @pl.when(band + k < bands)
            def _():
                columns = slice(j * piece, (j + 1) * piece)
                if j == 0:
                    coef_copy(k).wait_recv()
                panel_copy(k, j).wait_recv()
                mean, scale = coef_in[k - 1, 0:1, columns], coef_in[k - 1, 1:2, columns]

                def rescale(i, _):
                    span = pl.ds(pl.multiple_of(i * chunk, chunk), chunk)
                    window[k - 1, span, columns] = standard(window[k - 1, span, columns], mean, scale)
                    return 0

                lax.fori_loop(0, depth // chunk, rescale, 0)
                correlate(k, j, window.at[k - 1])

    for j in range(PIECES):
        finish(0, j)
    for j in range(PIECES):
        for k in range(1, reach + 1):
            @pl.when(band + k < bands)
            def _():
                finish(k, j)

            @pl.when(band + k >= bands)
            def _():
                place = slice(k * width + j * piece, k * width + (j + 1) * piece)
                out_ref[:, place] = jnp.zeros((rows, piece), jnp.float32)
    for k in range(1, reach + 1):
        @pl.when(band >= k)
        def _():
            coef_copy(k).wait_send()
            for j in range(PIECES):
                panel_copy(k, j).wait_send()


def on_device(bands, shards, dosage):
    depth, width = dosage.shape
    reach = (WIN - TILE + width - 1) // width
    rows = width // shards
    f32 = jnp.float32
    dma = pltpu.SemaphoreType.DMA
    return pl.pallas_call(
        functools.partial(kernel, bands, shards, reach, depth * shards),
        out_shape=jax.ShapeDtypeStruct((rows, WIN), f32),
        in_specs=[pl.BlockSpec(memory_space=pltpu.VMEM)],
        out_specs=pl.BlockSpec(memory_space=pltpu.VMEM),
        scratch_shapes=[
            pltpu.VMEM((width, depth), jnp.bfloat16),
            pltpu.VMEM((reach + 1, depth, width), jnp.bfloat16),
            pltpu.VMEM((8, width), f32),
            pltpu.VMEM((shards - 1, 8, width), f32),
            pltpu.VMEM((8, width), f32),
            pltpu.VMEM((reach, 8, width), f32),
            pltpu.VMEM((width, width // PIECES), f32),
            pltpu.VMEM((width, WIN), WIRE),
            pltpu.VMEM((shards - 1, rows, WIN), WIRE),
            dma((reach, PIECES)), dma((reach, PIECES)),
            dma((shards - 1,)), dma((shards - 1,)),
            dma((reach,)), dma((reach,)),
            dma((reach + 1, PIECES, shards - 1)), dma((reach + 1, PIECES, shards - 1)),
        ],
        compiler_params=pltpu.CompilerParams(
            collective_id=0, has_side_effects=True, vmem_limit_bytes=48 * 1024 * 1024
        ),
    )(dosage)


def solution(mesh):
    return jax.shard_map(
        functools.partial(on_device, mesh.shape["band"], mesh.shape["samp"]),
        mesh=mesh,
        in_specs=(P("samp", "band"),),
        out_specs=P(("band", "samp"), None),
        check_vma=False,
    )
```

```python
import functools

import jax
import jax.numpy as jnp
from jax import lax
from jax.experimental import pallas as pl
from jax.experimental.pallas import tpu as pltpu
from jax.sharding import PartitionSpec as P

TILE = 512
WIN = 2048
PIECES = 2
WIRE = jnp.float32
MESH = pl.DeviceIdType.MESH


def remote(src, dst, send, recv, band, samp):
    return pltpu.make_async_remote_copy(
        src_ref=src, dst_ref=dst, send_sem=send, recv_sem=recv,
        device_id=(band, samp), device_id_type=MESH,
    )


def kernel(bands, shards, reach, samples, raw_ref, out_ref, own_t, window, stats, stats_in, coef,
           coef_in, total_ref, parts, parts_in, panel_s, panel_r, stat_s, stat_r, coef_s, coef_r,
           part_s, part_r, relay_s, work):
    band = lax.axis_index("band")
    samp = lax.axis_index("samp")
    depth, width = raw_ref.shape
    rows = width // shards
    piece = width // PIECES
    peers = [lax.rem(samp + d, shards) for d in range(1, shards)]

    barrier = pltpu.get_barrier_semaphore()
    for peer in peers:
        pl.semaphore_signal(barrier, inc=1, device_id=(band, peer), device_id_type=MESH)
    expected = shards - 1
    for k in range(1, reach + 1):
        @pl.when(band >= k)
        def _():
            pl.semaphore_signal(barrier, inc=1, device_id=(band - k, samp), device_id_type=MESH)

        @pl.when(band + k < bands)
        def _():
            pl.semaphore_signal(barrier, inc=1, device_id=(band + k, samp), device_id_type=MESH)
    expected = expected + jnp.minimum(band, reach) + jnp.minimum(bands - 1 - band, reach)
    pl.semaphore_wait(barrier, expected)

    def panel_copy(k, j):
        columns = pl.ds(j * piece, piece)
        return remote(raw_ref.at[:, columns], window.at[k - 1, :, columns],
                      panel_s.at[k - 1, j], panel_r.at[k - 1, j], jnp.maximum(band - k, 0), samp)

    even = lax.rem(band, 2) == 0
    turn = lax.rem(band, 4)

    def sends(k):
        if k == 1:
            return jnp.logical_not(even)
        if k == 2:
            return (band >= 2) & (turn != 0)
        return even & (band >= 3)

    def relay_copy(k, j):
        columns = pl.ds(j * piece, piece)
        onward = (k == 2) & jnp.logical_not(even)
        target = jnp.clip(jnp.where(onward, band - 1, band + 1), 0, bands - 1)
        slot = jnp.where(k == 3, 1, jnp.where(even, 0, 2))
        return remote(window.at[k - 1, :, columns], window.at[slot, :, columns],
                      relay_s.at[k - 2, j], panel_r.at[slot, j], target, samp)

    def coef_copy(k):
        return remote(coef, coef_in.at[k - 1], coef_s.at[k - 1], coef_r.at[k - 1],
                      jnp.maximum(band - k, 0), samp)

    def part_copy(k, j, d):
        columns = pl.ds(pl.multiple_of(k * width + j * piece, piece), piece)
        return remote(parts.at[pl.ds(pl.multiple_of(peers[d] * rows, rows), rows), columns],
                      parts_in.at[d, :, columns],
                      part_s.at[k, j, d], part_r.at[k, j, d], band, peers[d])

    def start_panel(k, j):
        @pl.when(sends(k))
        def _():
            panel_copy(k, j).start()

    early = [(k, 0) for k in range(1, reach + 1)]
    later = [(k, j) for j in range(PIECES) for k in range(1, reach + 1) if (k, j) not in early]
    for k, j in early:
        start_panel(k, j)

    step = 64

    def add(i, carry):
        x = raw_ref[pl.ds(pl.multiple_of(i * step, step), step), :].astype(jnp.float32)
        seen = jnp.where(x >= 0.0, 1.0, 0.0)
        value = jnp.where(x >= 0.0, x, 0.0)
        fold = lambda a: jnp.sum(a.reshape(step // 8, 8, width), axis=0)
        return carry[0] + fold(seen), carry[1] + fold(value), carry[2] + fold(value * value)

    zero = jnp.zeros((8, width), jnp.float32)
    sums = lax.fori_loop(0, depth // step, add, (zero, zero, zero))
    stats[...] = jnp.concatenate(
        [jnp.sum(a, axis=0, keepdims=True) for a in sums] + [jnp.zeros((5, width), jnp.float32)], axis=0
    )
    stat_copies = [
        remote(stats, stats_in.at[d], stat_s.at[d], stat_r.at[d], band, peers[d])
        for d in range(shards - 1)
    ]
    for copy in stat_copies:
        copy.start()
    for copy in stat_copies:
        copy.wait()
    sums = stats[...]
    for d in range(shards - 1):
        sums = sums + stats_in[d]
    count, total, square = sums[0:1], sums[1:2], sums[2:3]
    mean = (total + 1.0) / (count + 1.0)
    spread = (square - 2.0 * mean * total + count * mean * mean + 0.5) / (count + 1.0)
    coef[...] = jnp.concatenate(
        [mean, lax.rsqrt(spread), jnp.zeros((6, width), jnp.float32)], axis=0
    )
    for k in range(1, reach + 1):
        @pl.when(band >= k)
        def _():
            coef_copy(k).start()
    for k, j in later:
        start_panel(k, j)

    chunk = 256

    def standard(x, mean, scale):
        x = x.astype(jnp.float32)
        return jnp.where(x >= 0.0, (x - mean) * scale, 0.0).astype(jnp.bfloat16)

    own = window.at[reach]

    def scale_own(i, _):
        span = pl.ds(pl.multiple_of(i * chunk, chunk), chunk)
        scaled = standard(raw_ref[span, :], coef[0:1, :], coef[1:2, :])
        own[span, :] = scaled
        own_t[:, span] = scaled.T
        return 0

    lax.fori_loop(0, depth // chunk, scale_own, 0)

    def correlate(k, j, panel):
        place = pl.ds(pl.multiple_of(k * width + j * piece, piece), piece)

        def block(i, _):
            span = pl.ds(pl.multiple_of(i * 256, 256), 256)
            total_ref[span, :] = jnp.dot(
                own_t[span, :], panel[...], preferred_element_type=jnp.float32
            )
            parts[span, place] = total_ref[span, :].astype(WIRE)
            return 0

        lax.fori_loop(0, width // 256, block, 0)
        for d in range(shards - 1):
            part_copy(k, j, d).start()
        out_ref[:, place] = total_ref[pl.ds(pl.multiple_of(samp * rows, rows), rows), :]

    def finish(k, j):
        place = slice(k * width + j * piece, k * width + (j + 1) * piece)
        total = out_ref[:, place]
        for d in range(shards - 1):
            part_copy(k, j, d).wait()
            total = total + parts_in[d, :, place].astype(jnp.float32)
        out_ref[:, place] = total / samples

    for j in range(PIECES):
        correlate(0, j, own.at[:, pl.ds(j * piece, piece)])
    for j in range(PIECES):
        columns = slice(j * piece, (j + 1) * piece)
        for t in range(reach):
            late = (t + 1) % reach + 1
            swapped = (1, 3, 2)[t]
            k = jnp.where(even, jnp.where(turn == 2, swapped, t + 1), late)

            @pl.when(band + k < bands)
            def _():
                panel_copy(k, j).wait_recv()

                @pl.when((k == 2) | ((k == 3) & (turn == 1)))
                def _():
                    relay_copy(k, j).start()

                if j == 0:
                    coef_copy(k).wait_recv()
                mean, scale = coef_in[k - 1, 0:1, columns], coef_in[k - 1, 1:2, columns]

                def rescale(i, _):
                    span = pl.ds(pl.multiple_of(i * chunk, chunk), chunk)
                    work[span, :] = standard(window[k - 1, span, columns], mean, scale)
                    return 0

                lax.fori_loop(0, depth // chunk, rescale, 0)
                correlate(k, j, work)

    for j in range(PIECES):
        finish(0, j)
    for j in range(PIECES):
        for k in range(1, reach + 1):
            @pl.when(band + k < bands)
            def _():
                finish(k, j)

            @pl.when(band + k >= bands)
            def _():
                place = slice(k * width + j * piece, k * width + (j + 1) * piece)
                out_ref[:, place] = jnp.zeros((rows, piece), jnp.float32)
    for k in range(1, reach + 1):
        @pl.when(band >= k)
        def _():
            coef_copy(k).wait_send()

        for j in range(PIECES):
            @pl.when(sends(k))
            def _():
                panel_copy(k, j).wait_send()

            if k > 1:
                @pl.when((band + k < bands) & ((k == 2) | (turn == 1)))
                def _():
                    relay_copy(k, j).wait_send()


def on_device(bands, shards, dosage):
    depth, width = dosage.shape
    reach = (WIN - TILE + width - 1) // width
    rows = width // shards
    f32 = jnp.float32
    dma = pltpu.SemaphoreType.DMA
    return pl.pallas_call(
        functools.partial(kernel, bands, shards, reach, depth * shards),
        out_shape=jax.ShapeDtypeStruct((rows, WIN), f32),
        in_specs=[pl.BlockSpec(memory_space=pltpu.VMEM)],
        out_specs=pl.BlockSpec(memory_space=pltpu.VMEM),
        scratch_shapes=[
            pltpu.VMEM((width, depth), jnp.bfloat16),
            pltpu.VMEM((reach + 1, depth, width), jnp.bfloat16),
            pltpu.VMEM((8, width), f32),
            pltpu.VMEM((shards - 1, 8, width), f32),
            pltpu.VMEM((8, width), f32),
            pltpu.VMEM((reach, 8, width), f32),
            pltpu.VMEM((width, width // PIECES), f32),
            pltpu.VMEM((width, WIN), WIRE),
            pltpu.VMEM((shards - 1, rows, WIN), WIRE),
            dma((reach, PIECES)), dma((reach, PIECES)),
            dma((shards - 1,)), dma((shards - 1,)),
            dma((reach,)), dma((reach,)),
            dma((reach + 1, PIECES, shards - 1)), dma((reach + 1, PIECES, shards - 1)),
            dma((reach - 1, PIECES)),
            pltpu.VMEM((depth, width // PIECES), jnp.bfloat16),
        ],
        compiler_params=pltpu.CompilerParams(
            collective_id=0, has_side_effects=True, vmem_limit_bytes=48 * 1024 * 1024
        ),
    )(dosage)


def solution(mesh):
    return jax.shard_map(
        functools.partial(on_device, mesh.shape["band"], mesh.shape["samp"]),
        mesh=mesh,
        in_specs=(P("samp", "band"),),
        out_specs=P(("band", "samp"), None),
        check_vma=False,
    )
```

```python
import functools

import jax
import jax.numpy as jnp
from jax import lax
from jax.experimental import pallas as pl
from jax.experimental.pallas import tpu as pltpu
from jax.sharding import PartitionSpec as P

TILE = 512
WIN = 2048
PIECES = 2
MESH = pl.DeviceIdType.MESH


def remote(src, dst, send, recv, band, samp):
    return pltpu.make_async_remote_copy(
        src_ref=src, dst_ref=dst, send_sem=send, recv_sem=recv,
        device_id=(band, samp), device_id_type=MESH,
    )


def kernel(bands, shards, reach, samples, raw_ref, out_ref, own_t, window, stats, stats_in, coef,
           coef_in, parts, far_parts, near_in, far_in, panel_s, panel_r, stat_s, stat_r, coef_s, coef_r,
           part_s, part_r, relay_s, work):
    band = lax.axis_index("band")
    samp = lax.axis_index("samp")
    depth, width = raw_ref.shape
    rows = width // shards
    piece = width // PIECES
    half = shards // 2
    side, seat = samp // half, lax.rem(samp, half)
    near = [side * half + lax.rem(seat + d, half) for d in range(1, half)]
    far = [(1 - side) * half + lax.rem(seat + d, half) for d in range(half)]
    peers = far + near

    barrier = pltpu.get_barrier_semaphore()
    for peer in peers:
        pl.semaphore_signal(barrier, inc=1, device_id=(band, peer), device_id_type=MESH)
    expected = shards - 1
    for k in range(1, reach + 1):
        @pl.when(band >= k)
        def _():
            pl.semaphore_signal(barrier, inc=1, device_id=(band - k, samp), device_id_type=MESH)

        @pl.when(band + k < bands)
        def _():
            pl.semaphore_signal(barrier, inc=1, device_id=(band + k, samp), device_id_type=MESH)
    expected = expected + jnp.minimum(band, reach) + jnp.minimum(bands - 1 - band, reach)
    pl.semaphore_wait(barrier, expected)

    def panel_copy(k, j):
        columns = pl.ds(j * piece, piece)
        return remote(raw_ref.at[:, columns], window.at[k - 1, :, columns],
                      panel_s.at[k - 1, j], panel_r.at[k - 1, j], jnp.maximum(band - k, 0), samp)

    even = lax.rem(band, 2) == 0
    turn = lax.rem(band, 4)

    def sends(k):
        if k == 1:
            return jnp.logical_not(even)
        if k == 2:
            return (band >= 2) & (turn != 0)
        return even & (band >= 3)

    def relay_copy(k, j):
        columns = pl.ds(j * piece, piece)
        onward = (k == 2) & jnp.logical_not(even)
        target = jnp.clip(jnp.where(onward, band - 1, band + 1), 0, bands - 1)
        slot = jnp.where(k == 3, 1, jnp.where(even, 0, 2))
        return remote(window.at[k - 1, :, columns], window.at[slot, :, columns],
                      relay_s.at[k - 2, j], panel_r.at[slot, j], target, samp)

    def coef_copy(k):
        return remote(coef, coef_in.at[k - 1], coef_s.at[k - 1], coef_r.at[k - 1],
                      jnp.maximum(band - k, 0), samp)

    def part_copy(k, j, d):
        columns = pl.ds(pl.multiple_of(k * width + j * piece, piece), piece)
        source, landing, slot = (far_parts, far_in, d) if d < half else (parts, near_in, d - half)
        return remote(source.at[pl.ds(pl.multiple_of(peers[d] * rows, rows), rows), columns],
                      landing.at[slot, :, columns],
                      part_s.at[k, j, d], part_r.at[k, j, d], band, peers[d])

    def start_panel(k, j):
        @pl.when(sends(k))
        def _():
            panel_copy(k, j).start()

    early = [(k, 0) for k in range(1, reach + 1)]
    later = [(k, j) for j in range(PIECES) for k in range(1, reach + 1) if (k, j) not in early]
    for k, j in early:
        start_panel(k, j)

    step = 64

    def add(i, carry):
        x = raw_ref[pl.ds(pl.multiple_of(i * step, step), step), :].astype(jnp.float32)
        seen = jnp.where(x >= 0.0, 1.0, 0.0)
        value = jnp.where(x >= 0.0, x, 0.0)
        fold = lambda a: jnp.sum(a.reshape(step // 8, 8, width), axis=0)
        return carry[0] + fold(seen), carry[1] + fold(value), carry[2] + fold(value * value)

    zero = jnp.zeros((8, width), jnp.float32)
    sums = lax.fori_loop(0, depth // step, add, (zero, zero, zero))
    stats[...] = jnp.concatenate(
        [jnp.sum(a, axis=0, keepdims=True) for a in sums] + [jnp.zeros((5, width), jnp.float32)], axis=0
    )
    stat_copies = [
        remote(stats, stats_in.at[d], stat_s.at[d], stat_r.at[d], band, peers[d])
        for d in range(shards - 1)
    ]
    for copy in stat_copies:
        copy.start()
    for copy in stat_copies:
        copy.wait()
    sums = stats[...]
    for d in range(shards - 1):
        sums = sums + stats_in[d]
    count, total, square = sums[0:1], sums[1:2], sums[2:3]
    mean = (total + 1.0) / (count + 1.0)
    spread = (square - 2.0 * mean * total + count * mean * mean + 0.5) / (count + 1.0)
    coef[...] = jnp.concatenate(
        [mean, lax.rsqrt(spread), jnp.zeros((6, width), jnp.float32)], axis=0
    )
    for k in range(1, reach + 1):
        @pl.when(band >= k)
        def _():
            coef_copy(k).start()
    for k, j in later:
        start_panel(k, j)

    chunk = 256

    def standard(x, mean, scale):
        x = x.astype(jnp.float32)
        return jnp.where(x >= 0.0, (x - mean) * scale, 0.0).astype(jnp.bfloat16)

    own = window.at[reach]

    def scale_own(i, _):
        span = pl.ds(pl.multiple_of(i * chunk, chunk), chunk)
        scaled = standard(raw_ref[span, :], coef[0:1, :], coef[1:2, :])
        own[span, :] = scaled
        own_t[:, span] = scaled.T
        return 0

    lax.fori_loop(0, depth // chunk, scale_own, 0)

    def correlate(k, j, panel):
        place = pl.ds(pl.multiple_of(k * width + j * piece, piece), piece)

        def block(i, _):
            span = pl.ds(pl.multiple_of(i * 256, 256), 256)
            total = jnp.dot(own_t[span, :], panel[...], preferred_element_type=jnp.float32)
            parts[span, place] = total
            far_parts[span, place] = total.astype(jnp.bfloat16)
            return 0

        lax.fori_loop(0, width // 256, block, 0)
        for d in range(shards - 1):
            part_copy(k, j, d).start()
        out_ref[:, place] = parts[pl.ds(pl.multiple_of(samp * rows, rows), rows), place]

    def finish(k, j):
        place = slice(k * width + j * piece, k * width + (j + 1) * piece)
        total = out_ref[:, place]
        for d in range(shards - 1):
            part_copy(k, j, d).wait()
            landed = far_in[d, :, place] if d < half else near_in[d - half, :, place]
            total = total + landed.astype(jnp.float32)
        out_ref[:, place] = total / samples

    for j in range(PIECES):
        correlate(0, j, own.at[:, pl.ds(j * piece, piece)])
    for j in range(PIECES):
        columns = slice(j * piece, (j + 1) * piece)
        for t in range(reach):
            late = (t + 1) % reach + 1
            swapped = (1, 3, 2)[t]
            k = jnp.where(even, jnp.where(turn == 2, swapped, t + 1), late)

            @pl.when(band + k < bands)
            def _():
                panel_copy(k, j).wait_recv()

                @pl.when((k == 2) | ((k == 3) & (turn == 1)))
                def _():
                    relay_copy(k, j).start()

                if j == 0:
                    coef_copy(k).wait_recv()
                mean, scale = coef_in[k - 1, 0:1, columns], coef_in[k - 1, 1:2, columns]

                def rescale(i, _):
                    span = pl.ds(pl.multiple_of(i * chunk, chunk), chunk)
                    work[span, :] = standard(window[k - 1, span, columns], mean, scale)
                    return 0

                lax.fori_loop(0, depth // chunk, rescale, 0)
                correlate(k, j, work)

    for j in range(PIECES):
        finish(0, j)
    for j in range(PIECES):
        for k in range(1, reach + 1):
            @pl.when(band + k < bands)
            def _():
                finish(k, j)

            @pl.when(band + k >= bands)
            def _():
                place = slice(k * width + j * piece, k * width + (j + 1) * piece)
                out_ref[:, place] = jnp.zeros((rows, piece), jnp.float32)
    for k in range(1, reach + 1):
        @pl.when(band >= k)
        def _():
            coef_copy(k).wait_send()

        for j in range(PIECES):
            @pl.when(sends(k))
            def _():
                panel_copy(k, j).wait_send()

            if k > 1:
                @pl.when((band + k < bands) & ((k == 2) | (turn == 1)))
                def _():
                    relay_copy(k, j).wait_send()


def on_device(bands, shards, dosage):
    depth, width = dosage.shape
    reach = (WIN - TILE + width - 1) // width
    rows = width // shards
    f32 = jnp.float32
    dma = pltpu.SemaphoreType.DMA
    return pl.pallas_call(
        functools.partial(kernel, bands, shards, reach, depth * shards),
        out_shape=jax.ShapeDtypeStruct((rows, WIN), f32),
        in_specs=[pl.BlockSpec(memory_space=pltpu.VMEM)],
        out_specs=pl.BlockSpec(memory_space=pltpu.VMEM),
        scratch_shapes=[
            pltpu.VMEM((width, depth), jnp.bfloat16),
            pltpu.VMEM((reach + 1, depth, width), jnp.bfloat16),
            pltpu.VMEM((8, width), f32),
            pltpu.VMEM((shards - 1, 8, width), f32),
            pltpu.VMEM((8, width), f32),
            pltpu.VMEM((reach, 8, width), f32),
            pltpu.VMEM((width, WIN), f32),
            pltpu.VMEM((width, WIN), jnp.bfloat16),
            pltpu.VMEM((max(shards // 2 - 1, 1), rows, WIN), f32),
            pltpu.VMEM((shards // 2, rows, WIN), jnp.bfloat16),
            dma((reach, PIECES)), dma((reach, PIECES)),
            dma((shards - 1,)), dma((shards - 1,)),
            dma((reach,)), dma((reach,)),
            dma((reach + 1, PIECES, shards - 1)), dma((reach + 1, PIECES, shards - 1)),
            dma((reach - 1, PIECES)),
            pltpu.VMEM((depth, width // PIECES), jnp.bfloat16),
        ],
        compiler_params=pltpu.CompilerParams(
            collective_id=0, has_side_effects=True, vmem_limit_bytes=48 * 1024 * 1024
        ),
    )(dosage)


def solution(mesh):
    return jax.shard_map(
        functools.partial(on_device, mesh.shape["band"], mesh.shape["samp"]),
        mesh=mesh,
        in_specs=(P("samp", "band"),),
        out_specs=P(("band", "samp"), None),
        check_vma=False,
    )
```

```python
import functools

import jax
import jax.numpy as jnp
from jax import lax
from jax.experimental import pallas as pl
from jax.experimental.pallas import tpu as pltpu
from jax.sharding import PartitionSpec as P

TILE = 512
WIN = 2048
PIECES = 4
MESH = pl.DeviceIdType.MESH


def remote(src, dst, send, recv, band, samp):
    return pltpu.make_async_remote_copy(
        src_ref=src, dst_ref=dst, send_sem=send, recv_sem=recv,
        device_id=(band, samp), device_id_type=MESH,
    )


def kernel(bands, shards, reach, samples, raw_ref, out_ref, own_t, window, stats, stats_in, coef,
           coef_in, parts, far_parts, near_in, far_in, panel_s, panel_r, stat_s, stat_r, coef_s, coef_r,
           part_s, part_r, relay_s, work):
    band = lax.axis_index("band")
    samp = lax.axis_index("samp")
    depth, width = raw_ref.shape
    rows = width // shards
    piece = width // PIECES
    half = shards // 2
    side, seat = samp // half, lax.rem(samp, half)
    near = [side * half + lax.rem(seat + d, half) for d in range(1, half)]
    far = [(1 - side) * half + lax.rem(seat + d, half) for d in range(half)]
    peers = far + near

    barrier = pltpu.get_barrier_semaphore()
    for peer in peers:
        pl.semaphore_signal(barrier, inc=1, device_id=(band, peer), device_id_type=MESH)
    expected = shards - 1
    for k in range(1, reach + 1):
        @pl.when(band >= k)
        def _():
            pl.semaphore_signal(barrier, inc=1, device_id=(band - k, samp), device_id_type=MESH)

        @pl.when(band + k < bands)
        def _():
            pl.semaphore_signal(barrier, inc=1, device_id=(band + k, samp), device_id_type=MESH)
    expected = expected + jnp.minimum(band, reach) + jnp.minimum(bands - 1 - band, reach)
    pl.semaphore_wait(barrier, expected)

    def panel_copy(k, j):
        columns = pl.ds(j * piece, piece)
        return remote(raw_ref.at[:, columns], window.at[k - 1, :, columns],
                      panel_s.at[k - 1, j], panel_r.at[k - 1, j], jnp.maximum(band - k, 0), samp)

    even = lax.rem(band, 2) == 0
    turn = lax.rem(band, 4)

    def sends(k):
        if k == 1:
            return jnp.logical_not(even)
        if k == 2:
            return (band >= 2) & (turn != 0)
        return even & (band >= 3)

    def relay_copy(k, j):
        columns = pl.ds(j * piece, piece)
        onward = (k == 2) & jnp.logical_not(even)
        target = jnp.clip(jnp.where(onward, band - 1, band + 1), 0, bands - 1)
        slot = jnp.where(k == 3, 1, jnp.where(even, 0, 2))
        return remote(window.at[k - 1, :, columns], window.at[slot, :, columns],
                      relay_s.at[k - 2, j], panel_r.at[slot, j], target, samp)

    def coef_copy(k):
        return remote(coef, coef_in.at[k - 1], coef_s.at[k - 1], coef_r.at[k - 1],
                      jnp.maximum(band - k, 0), samp)

    def part_copy(k, j, d):
        columns = pl.ds(pl.multiple_of(k * width + j * piece, piece), piece)
        source, landing, slot = (far_parts, far_in, d) if d < half else (parts, near_in, d - half)
        return remote(source.at[pl.ds(pl.multiple_of(peers[d] * rows, rows), rows), columns],
                      landing.at[slot, :, columns],
                      part_s.at[k, j, d], part_r.at[k, j, d], band, peers[d])

    def start_panel(k, j):
        @pl.when(sends(k))
        def _():
            panel_copy(k, j).start()

    early = [(k, 0) for k in range(1, reach + 1)]
    later = [(k, j) for j in range(PIECES) for k in range(1, reach + 1) if (k, j) not in early]
    for k, j in early:
        start_panel(k, j)

    step = 64

    def add(i, carry):
        x = raw_ref[pl.ds(pl.multiple_of(i * step, step), step), :].astype(jnp.float32)
        seen = jnp.where(x >= 0.0, 1.0, 0.0)
        value = jnp.where(x >= 0.0, x, 0.0)
        fold = lambda a: jnp.sum(a.reshape(step // 8, 8, width), axis=0)
        return carry[0] + fold(seen), carry[1] + fold(value), carry[2] + fold(value * value)

    zero = jnp.zeros((8, width), jnp.float32)
    sums = lax.fori_loop(0, depth // step, add, (zero, zero, zero))
    stats[...] = jnp.concatenate(
        [jnp.sum(a, axis=0, keepdims=True) for a in sums] + [jnp.zeros((5, width), jnp.float32)], axis=0
    )
    stat_copies = [
        remote(stats, stats_in.at[d], stat_s.at[d], stat_r.at[d], band, peers[d])
        for d in range(shards - 1)
    ]
    for copy in stat_copies:
        copy.start()
    for copy in stat_copies:
        copy.wait()
    sums = stats[...]
    for d in range(shards - 1):
        sums = sums + stats_in[d]
    count, total, square = sums[0:1], sums[1:2], sums[2:3]
    mean = (total + 1.0) / (count + 1.0)
    spread = (square - 2.0 * mean * total + count * mean * mean + 0.5) / (count + 1.0)
    coef[...] = jnp.concatenate(
        [mean, lax.rsqrt(spread), jnp.zeros((6, width), jnp.float32)], axis=0
    )
    for k in range(1, reach + 1):
        @pl.when(band >= k)
        def _():
            coef_copy(k).start()
    for k, j in later:
        start_panel(k, j)

    chunk = 256

    def standard(x, mean, scale):
        x = x.astype(jnp.float32)
        return jnp.where(x >= 0.0, (x - mean) * scale, 0.0).astype(jnp.bfloat16)

    own = window.at[reach]

    def scale_own(i, _):
        span = pl.ds(pl.multiple_of(i * chunk, chunk), chunk)
        scaled = standard(raw_ref[span, :], coef[0:1, :], coef[1:2, :])
        own[span, :] = scaled
        own_t[:, span] = scaled.T
        return 0

    lax.fori_loop(0, depth // chunk, scale_own, 0)

    def correlate(k, j, panel):
        place = pl.ds(pl.multiple_of(k * width + j * piece, piece), piece)

        def block(i, _):
            span = pl.ds(pl.multiple_of(i * 256, 256), 256)
            total = jnp.dot(own_t[span, :], panel[...], preferred_element_type=jnp.float32)
            parts[span, place] = total
            far_parts[span, place] = total.astype(jnp.bfloat16)
            return 0

        lax.fori_loop(0, width // 256, block, 0)
        for d in range(shards - 1):
            part_copy(k, j, d).start()
        out_ref[:, place] = parts[pl.ds(pl.multiple_of(samp * rows, rows), rows), place]

    def finish(k, j):
        place = slice(k * width + j * piece, k * width + (j + 1) * piece)
        total = out_ref[:, place]
        for d in range(shards - 1):
            part_copy(k, j, d).wait()
            landed = far_in[d, :, place] if d < half else near_in[d - half, :, place]
            total = total + landed.astype(jnp.float32)
        out_ref[:, place] = total / samples

    for j in range(PIECES):
        correlate(0, j, own.at[:, pl.ds(j * piece, piece)])
    for j in range(PIECES):
        columns = slice(j * piece, (j + 1) * piece)
        for t in range(reach):
            late = (t + 1) % reach + 1
            swapped = (1, 3, 2)[t]
            k = jnp.where(even, jnp.where(turn == 2, swapped, t + 1), late)

            @pl.when(band + k < bands)
            def _():
                panel_copy(k, j).wait_recv()

                @pl.when((k == 2) | ((k == 3) & (turn == 1)))
                def _():
                    relay_copy(k, j).start()

                if j == 0:
                    coef_copy(k).wait_recv()
                mean, scale = coef_in[k - 1, 0:1, columns], coef_in[k - 1, 1:2, columns]

                def rescale(i, _):
                    span = pl.ds(pl.multiple_of(i * chunk, chunk), chunk)
                    work[span, :] = standard(window[k - 1, span, columns], mean, scale)
                    return 0

                lax.fori_loop(0, depth // chunk, rescale, 0)
                correlate(k, j, work)

    for j in range(PIECES):
        finish(0, j)
    for j in range(PIECES):
        for k in range(1, reach + 1):
            @pl.when(band + k < bands)
            def _():
                finish(k, j)

            @pl.when(band + k >= bands)
            def _():
                place = slice(k * width + j * piece, k * width + (j + 1) * piece)
                out_ref[:, place] = jnp.zeros((rows, piece), jnp.float32)
    for k in range(1, reach + 1):
        @pl.when(band >= k)
        def _():
            coef_copy(k).wait_send()

        for j in range(PIECES):
            @pl.when(sends(k))
            def _():
                panel_copy(k, j).wait_send()

            if k > 1:
                @pl.when((band + k < bands) & ((k == 2) | (turn == 1)))
                def _():
                    relay_copy(k, j).wait_send()


def on_device(bands, shards, dosage):
    depth, width = dosage.shape
    reach = (WIN - TILE + width - 1) // width
    rows = width // shards
    f32 = jnp.float32
    dma = pltpu.SemaphoreType.DMA
    return pl.pallas_call(
        functools.partial(kernel, bands, shards, reach, depth * shards),
        out_shape=jax.ShapeDtypeStruct((rows, WIN), f32),
        in_specs=[pl.BlockSpec(memory_space=pltpu.VMEM)],
        out_specs=pl.BlockSpec(memory_space=pltpu.VMEM),
        scratch_shapes=[
            pltpu.VMEM((width, depth), jnp.bfloat16),
            pltpu.VMEM((reach + 1, depth, width), jnp.bfloat16),
            pltpu.VMEM((8, width), f32),
            pltpu.VMEM((shards - 1, 8, width), f32),
            pltpu.VMEM((8, width), f32),
            pltpu.VMEM((reach, 8, width), f32),
            pltpu.VMEM((width, WIN), f32),
            pltpu.VMEM((width, WIN), jnp.bfloat16),
            pltpu.VMEM((max(shards // 2 - 1, 1), rows, WIN), f32),
            pltpu.VMEM((shards // 2, rows, WIN), jnp.bfloat16),
            dma((reach, PIECES)), dma((reach, PIECES)),
            dma((shards - 1,)), dma((shards - 1,)),
            dma((reach,)), dma((reach,)),
            dma((reach + 1, PIECES, shards - 1)), dma((reach + 1, PIECES, shards - 1)),
            dma((reach - 1, PIECES)),
            pltpu.VMEM((depth, width // PIECES), jnp.bfloat16),
        ],
        compiler_params=pltpu.CompilerParams(
            collective_id=0, has_side_effects=True, vmem_limit_bytes=48 * 1024 * 1024
        ),
    )(dosage)


def solution(mesh):
    return jax.shard_map(
        functools.partial(on_device, mesh.shape["band"], mesh.shape["samp"]),
        mesh=mesh,
        in_specs=(P("samp", "band"),),
        out_specs=P(("band", "samp"), None),
        check_vma=False,
    )
```

```python
import functools

import jax
import jax.numpy as jnp
from jax import lax
from jax.experimental import pallas as pl
from jax.experimental.pallas import tpu as pltpu
from jax.sharding import PartitionSpec as P

TILE = 512
WIN = 2048
PIECES = 4
MESH = pl.DeviceIdType.MESH


def remote(src, dst, send, recv, band, samp):
    return pltpu.make_async_remote_copy(
        src_ref=src, dst_ref=dst, send_sem=send, recv_sem=recv,
        device_id=(band, samp), device_id_type=MESH,
    )


def kernel(bands, shards, reach, samples, dosage_ref, out_ref, own_t, window, stats, stats_in, coef,
           coef_in, parts, far_parts, near_in, far_in, panel_s, panel_r, stat_s, stat_r, coef_s, coef_r,
           part_s, part_r, relay_s, work, raw_ref, load_s):
    band = lax.axis_index("band")
    samp = lax.axis_index("samp")
    depth, width = raw_ref.shape
    load = pltpu.make_async_copy(dosage_ref, raw_ref, load_s)
    load.start()
    rows = width // shards
    piece = width // PIECES
    half = shards // 2
    side, seat = samp // half, lax.rem(samp, half)
    near = [side * half + lax.rem(seat + d, half) for d in range(1, half)]
    far = [(1 - side) * half + lax.rem(seat + d, half) for d in range(half)]
    peers = far + near

    barrier = pltpu.get_barrier_semaphore()
    for peer in peers:
        pl.semaphore_signal(barrier, inc=1, device_id=(band, peer), device_id_type=MESH)
    expected = shards - 1
    for k in range(1, reach + 1):
        @pl.when(band >= k)
        def _():
            pl.semaphore_signal(barrier, inc=1, device_id=(band - k, samp), device_id_type=MESH)

        @pl.when(band + k < bands)
        def _():
            pl.semaphore_signal(barrier, inc=1, device_id=(band + k, samp), device_id_type=MESH)
    expected = expected + jnp.minimum(band, reach) + jnp.minimum(bands - 1 - band, reach)
    pl.semaphore_wait(barrier, expected)
    load.wait()

    def panel_copy(k, j):
        columns = pl.ds(pl.multiple_of(j * piece, piece), piece)
        return remote(raw_ref.at[:, columns], window.at[k - 1, :, columns],
                      panel_s.at[k - 1, j], panel_r.at[k - 1, j], jnp.maximum(band - k, 0), samp)

    even = lax.rem(band, 2) == 0
    turn = lax.rem(band, 4)

    def sends(k):
        if k == 1:
            return jnp.logical_not(even)
        if k == 2:
            return (band >= 2) & (turn != 0)
        return even & (band >= 3)

    def relay_copy(k, j):
        columns = pl.ds(pl.multiple_of(j * piece, piece), piece)
        onward = (k == 2) & jnp.logical_not(even)
        target = jnp.clip(jnp.where(onward, band - 1, band + 1), 0, bands - 1)
        slot = jnp.where(k == 3, 1, jnp.where(even, 0, 2))
        return remote(window.at[k - 1, :, columns], window.at[slot, :, columns],
                      relay_s.at[k - 2, j], panel_r.at[slot, j], target, samp)

    def coef_copy(k):
        return remote(coef, coef_in.at[k - 1], coef_s.at[k - 1], coef_r.at[k - 1],
                      jnp.maximum(band - k, 0), samp)

    def part_copy(k, j, d):
        columns = pl.ds(pl.multiple_of(k * width + j * piece, piece), piece)
        source, landing, slot = (far_parts, far_in, d) if d < half else (parts, near_in, d - half)
        return remote(source.at[pl.ds(pl.multiple_of(peers[d] * rows, rows), rows), columns],
                      landing.at[slot, :, columns],
                      part_s.at[k, j, d], part_r.at[k, j, d], band, peers[d])

    def start_panel(k, j):
        @pl.when(sends(k))
        def _():
            panel_copy(k, j).start()

    early = [(k, 0) for k in range(1, reach + 1)]
    later = [(k, j) for j in range(PIECES) for k in range(1, reach + 1) if (k, j) not in early]
    for k, j in early:
        start_panel(k, j)

    step = 64

    def add(i, carry):
        x = raw_ref[pl.ds(pl.multiple_of(i * step, step), step), :].astype(jnp.float32)
        seen = jnp.where(x >= 0.0, 1.0, 0.0)
        value = jnp.where(x >= 0.0, x, 0.0)
        fold = lambda a: jnp.sum(a.reshape(step // 8, 8, width), axis=0)
        return carry[0] + fold(seen), carry[1] + fold(value), carry[2] + fold(value * value)

    zero = jnp.zeros((8, width), jnp.float32)
    sums = lax.fori_loop(0, depth // step, add, (zero, zero, zero))
    stats[...] = jnp.concatenate(
        [jnp.sum(a, axis=0, keepdims=True) for a in sums] + [jnp.zeros((5, width), jnp.float32)], axis=0
    )
    stat_copies = [
        remote(stats, stats_in.at[d], stat_s.at[d], stat_r.at[d], band, peers[d])
        for d in range(shards - 1)
    ]
    for copy in stat_copies:
        copy.start()
    for copy in stat_copies:
        copy.wait()
    sums = stats[...]
    for d in range(shards - 1):
        sums = sums + stats_in[d]
    count, total, square = sums[0:1], sums[1:2], sums[2:3]
    mean = (total + 1.0) / (count + 1.0)
    spread = (square - 2.0 * mean * total + count * mean * mean + 0.5) / (count + 1.0)
    coef[...] = jnp.concatenate(
        [mean, lax.rsqrt(spread), jnp.zeros((6, width), jnp.float32)], axis=0
    )
    for k in range(1, reach + 1):
        @pl.when(band >= k)
        def _():
            coef_copy(k).start()
    for k, j in later:
        start_panel(k, j)

    chunk = 256

    def standard(x, mean, scale):
        x = x.astype(jnp.float32)
        return jnp.where(x >= 0.0, (x - mean) * scale, 0.0).astype(jnp.bfloat16)

    own = window.at[reach]

    def scale_own(i, _):
        span = pl.ds(pl.multiple_of(i * chunk, chunk), chunk)
        scaled = standard(raw_ref[span, :], coef[0:1, :], coef[1:2, :])
        own[span, :] = scaled
        own_t[:, span] = scaled.T
        return 0

    lax.fori_loop(0, depth // chunk, scale_own, 0)

    def correlate(k, j, panel):
        place = pl.ds(pl.multiple_of(k * width + j * piece, piece), piece)

        def block(i, _):
            span = pl.ds(pl.multiple_of(i * 256, 256), 256)
            total = jnp.dot(own_t[span, :], panel[...], preferred_element_type=jnp.float32)
            parts[span, place] = total
            far_parts[span, place] = total.astype(jnp.bfloat16)
            return 0

        lax.fori_loop(0, width // 256, block, 0)
        for d in range(shards - 1):
            part_copy(k, j, d).start()
        out_ref[:, place] = parts[pl.ds(pl.multiple_of(samp * rows, rows), rows), place]

    def finish(k, j):
        place = slice(k * width + j * piece, k * width + (j + 1) * piece)
        total = out_ref[:, place]
        for d in range(shards - 1):
            part_copy(k, j, d).wait()
            landed = far_in[d, :, place] if d < half else near_in[d - half, :, place]
            total = total + landed.astype(jnp.float32)
        out_ref[:, place] = total / samples

    for j in range(PIECES):
        correlate(0, j, own.at[:, pl.ds(j * piece, piece)])
    ahead = [(1, 0)]
    for j in range(PIECES):
        ahead += [(1, j + 1)] if j + 1 < PIECES else []
        ahead += [(k, j) for k in range(2, reach + 1)]
    level = [(k, j) for j in range(PIECES) for k in range(reach, 0, -1)]
    for (k_even, j_even), (k_odd, j_odd) in zip(ahead, level):
        k_relayed = k_even if k_even == 1 else reach + 2 - k_even
        k = jnp.where(even, jnp.where(turn == 2, k_relayed, k_even), k_odd)
        j = jnp.where(even, j_even, j_odd)
        columns = pl.ds(pl.multiple_of(j * piece, piece), piece)

        @pl.when(band + k < bands)
        def _():
            panel_copy(k, j).wait_recv()

            @pl.when((k == 2) | ((k == 3) & (turn == 1)))
            def _():
                relay_copy(k, j).start()

            @pl.when(j == 0)
            def _():
                coef_copy(k).wait_recv()

            mean, scale = coef_in[k - 1, 0:1, columns], coef_in[k - 1, 1:2, columns]

            def rescale(i, _):
                span = pl.ds(pl.multiple_of(i * chunk, chunk), chunk)
                work[span, :] = standard(window[k - 1, span, columns], mean, scale)
                return 0

            lax.fori_loop(0, depth // chunk, rescale, 0)
            correlate(k, j, work)

    for j in range(PIECES):
        finish(0, j)
    for j in range(PIECES):
        for k in range(1, reach + 1):
            @pl.when(band + k < bands)
            def _():
                finish(k, j)

            @pl.when(band + k >= bands)
            def _():
                place = slice(k * width + j * piece, k * width + (j + 1) * piece)
                out_ref[:, place] = jnp.zeros((rows, piece), jnp.float32)
    for k in range(1, reach + 1):
        @pl.when(band >= k)
        def _():
            coef_copy(k).wait_send()

        for j in range(PIECES):
            @pl.when(sends(k))
            def _():
                panel_copy(k, j).wait_send()

            if k > 1:
                @pl.when((band + k < bands) & ((k == 2) | (turn == 1)))
                def _():
                    relay_copy(k, j).wait_send()


def on_device(bands, shards, dosage):
    depth, width = dosage.shape
    reach = (WIN - TILE + width - 1) // width
    rows = width // shards
    f32 = jnp.float32
    dma = pltpu.SemaphoreType.DMA
    return pl.pallas_call(
        functools.partial(kernel, bands, shards, reach, depth * shards),
        out_shape=jax.ShapeDtypeStruct((rows, WIN), f32),
        in_specs=[pl.BlockSpec(memory_space=pltpu.HBM)],
        out_specs=pl.BlockSpec(memory_space=pltpu.VMEM),
        scratch_shapes=[
            pltpu.VMEM((width, depth), jnp.bfloat16),
            pltpu.VMEM((reach + 1, depth, width), jnp.bfloat16),
            pltpu.VMEM((8, width), f32),
            pltpu.VMEM((shards - 1, 8, width), f32),
            pltpu.VMEM((8, width), f32),
            pltpu.VMEM((reach, 8, width), f32),
            pltpu.VMEM((width, WIN), f32),
            pltpu.VMEM((width, WIN), jnp.bfloat16),
            pltpu.VMEM((max(shards // 2 - 1, 1), rows, WIN), f32),
            pltpu.VMEM((shards // 2, rows, WIN), jnp.bfloat16),
            dma((reach, PIECES)), dma((reach, PIECES)),
            dma((shards - 1,)), dma((shards - 1,)),
            dma((reach,)), dma((reach,)),
            dma((reach + 1, PIECES, shards - 1)), dma((reach + 1, PIECES, shards - 1)),
            dma((reach - 1, PIECES)),
            pltpu.VMEM((depth, width // PIECES), jnp.bfloat16),
            pltpu.VMEM((depth, width), jnp.bfloat16),
            dma(()),
        ],
        compiler_params=pltpu.CompilerParams(
            collective_id=0, has_side_effects=True, vmem_limit_bytes=48 * 1024 * 1024
        ),
    )(dosage)


def solution(mesh):
    return jax.shard_map(
        functools.partial(on_device, mesh.shape["band"], mesh.shape["samp"]),
        mesh=mesh,
        in_specs=(P("samp", "band"),),
        out_specs=P(("band", "samp"), None),
        check_vma=False,
    )
```

```python
import functools

import jax
import jax.numpy as jnp
from jax import lax
from jax.experimental import pallas as pl
from jax.experimental.pallas import tpu as pltpu
from jax.sharding import PartitionSpec as P

TILE = 512
WIN = 2048
PIECES = 4
MESH = pl.DeviceIdType.MESH


def remote(src, dst, send, recv, band, samp):
    return pltpu.make_async_remote_copy(
        src_ref=src, dst_ref=dst, send_sem=send, recv_sem=recv,
        device_id=(band, samp), device_id_type=MESH,
    )


def kernel(bands, shards, reach, samples, dosage_ref, out_ref, own_t, window, stats, stats_in, coef,
           coef_in, parts, far_parts, near_in, far_in, panel_s, panel_r, stat_s, stat_r, coef_s, coef_r,
           part_s, part_r, relay_s, work, raw_ref, load_s):
    band = lax.axis_index("band")
    samp = lax.axis_index("samp")
    depth, width = raw_ref.shape
    load = pltpu.make_async_copy(dosage_ref, raw_ref, load_s)
    load.start()
    rows = width // shards
    piece = width // PIECES
    half = shards // 2
    side, seat = samp // half, lax.rem(samp, half)
    near = [side * half + lax.rem(seat + d, half) for d in range(1, half)]
    far = [(1 - side) * half + lax.rem(seat + d, half) for d in range(half)]
    peers = far + near

    barrier = pltpu.get_barrier_semaphore()
    for peer in peers:
        pl.semaphore_signal(barrier, inc=1, device_id=(band, peer), device_id_type=MESH)
    expected = shards - 1
    for k in range(1, reach + 1):
        @pl.when(band >= k)
        def _():
            pl.semaphore_signal(barrier, inc=1, device_id=(band - k, samp), device_id_type=MESH)

        @pl.when(band + k < bands)
        def _():
            pl.semaphore_signal(barrier, inc=1, device_id=(band + k, samp), device_id_type=MESH)
    expected = expected + jnp.minimum(band, reach) + jnp.minimum(bands - 1 - band, reach)
    pl.semaphore_wait(barrier, expected)
    load.wait()

    def panel_copy(k, j):
        columns = pl.ds(pl.multiple_of(j * piece, piece), piece)
        return remote(raw_ref.at[:, columns], window.at[k - 1, :, columns],
                      panel_s.at[k - 1, j], panel_r.at[k - 1, j], jnp.maximum(band - k, 0), samp)

    even = lax.rem(band, 2) == 0
    turn = lax.rem(band, 4)

    def sends(k):
        if k == 1:
            return jnp.logical_not(even)
        if k == 2:
            return (band >= 2) & (turn != 0)
        return even & (band >= 3)

    def relay_copy(k, j):
        columns = pl.ds(pl.multiple_of(j * piece, piece), piece)
        onward = (k == 2) & jnp.logical_not(even)
        target = jnp.clip(jnp.where(onward, band - 1, band + 1), 0, bands - 1)
        slot = jnp.where(k == 3, 1, jnp.where(even, 0, 2))
        return remote(window.at[k - 1, :, columns], window.at[slot, :, columns],
                      relay_s.at[k - 2, j], panel_r.at[slot, j], target, samp)

    def coef_copy(k):
        return remote(coef, coef_in.at[k - 1], coef_s.at[k - 1], coef_r.at[k - 1],
                      jnp.maximum(band - k, 0), samp)

    def part_copy(k, j, d):
        columns = pl.ds(pl.multiple_of(k * width + j * piece, piece), piece)
        source, landing, slot = (far_parts, far_in, d) if d < half else (parts, near_in, d - half)
        return remote(source.at[pl.ds(pl.multiple_of(peers[d] * rows, rows), rows), columns],
                      landing.at[slot, :, columns],
                      part_s.at[k, j, d], part_r.at[k, j, d], band, peers[d])

    def start_panel(k, j):
        @pl.when(sends(k))
        def _():
            panel_copy(k, j).start()

    early = [(k, 0) for k in range(1, reach + 1)]
    later = [(k, j) for j in range(PIECES) for k in range(1, reach + 1) if (k, j) not in early]
    for k, j in early:
        start_panel(k, j)

    step = 64

    def add(i, carry):
        x = raw_ref[pl.ds(pl.multiple_of(i * step, step), step), :].astype(jnp.float32)
        seen = jnp.where(x >= 0.0, 1.0, 0.0)
        value = jnp.where(x >= 0.0, x, 0.0)
        fold = lambda a: jnp.sum(a.reshape(step // 8, 8, width), axis=0)
        return carry[0] + fold(seen), carry[1] + fold(value), carry[2] + fold(value * value)

    zero = jnp.zeros((8, width), jnp.float32)
    sums = lax.fori_loop(0, depth // step, add, (zero, zero, zero))
    stats[...] = jnp.concatenate(
        [jnp.sum(a, axis=0, keepdims=True) for a in sums] + [jnp.zeros((5, width), jnp.float32)], axis=0
    )
    stat_copies = [
        remote(stats, stats_in.at[d], stat_s.at[d], stat_r.at[d], band, peers[d])
        for d in range(shards - 1)
    ]
    for copy in stat_copies:
        copy.start()
    for copy in stat_copies:
        copy.wait()
    sums = stats[...]
    for d in range(shards - 1):
        sums = sums + stats_in[d]
    count, total, square = sums[0:1], sums[1:2], sums[2:3]
    mean = (total + 1.0) / (count + 1.0)
    spread = (square - 2.0 * mean * total + count * mean * mean + 0.5) / (count + 1.0)
    coef[...] = jnp.concatenate(
        [mean, lax.rsqrt(spread), jnp.zeros((6, width), jnp.float32)], axis=0
    )
    for k in range(1, reach + 1):
        @pl.when(band >= k)
        def _():
            coef_copy(k).start()
    for k, j in later:
        start_panel(k, j)

    chunk = 256

    def standard(x, mean, scale):
        x = x.astype(jnp.float32)
        return jnp.where(x >= 0.0, (x - mean) * scale, 0.0).astype(jnp.bfloat16)

    own = window.at[reach]

    def scale_own(i, _):
        span = pl.ds(pl.multiple_of(i * chunk, chunk), chunk)
        scaled = standard(raw_ref[span, :], coef[0:1, :], coef[1:2, :])
        own[span, :] = scaled
        own_t[:, span] = scaled.T
        return 0

    lax.fori_loop(0, depth // chunk, scale_own, 0)

    def correlate(k, j, panel):
        place = pl.ds(pl.multiple_of(k * width + j * piece, piece), piece)

        def block(i, _):
            span = pl.ds(pl.multiple_of(i * 256, 256), 256)
            total = jnp.dot(own_t[span, :], panel[...], preferred_element_type=jnp.float32)
            parts[span, place] = total
            far_parts[span, place] = total.astype(jnp.bfloat16)
            return 0

        lax.fori_loop(0, width // 256, block, 0)
        for d in range(shards - 1):
            part_copy(k, j, d).start()
        out_ref[:, place] = parts[pl.ds(pl.multiple_of(samp * rows, rows), rows), place]

    def finish(k, j):
        place = slice(k * width + j * piece, k * width + (j + 1) * piece)
        total = out_ref[:, place]
        for d in range(shards - 1):
            part_copy(k, j, d).wait()
            landed = far_in[d, :, place] if d < half else near_in[d - half, :, place]
            total = total + landed.astype(jnp.float32)
        out_ref[:, place] = total / samples

    for j in range(PIECES):
        correlate(0, j, own.at[:, pl.ds(j * piece, piece)])
    ahead = [(1, 0)]
    for j in range(PIECES):
        ahead += [(1, j + 1)] if j + 1 < PIECES else []
        ahead += [(k, j) for k in range(2, reach + 1)]
    level = [(k, j) for j in range(PIECES) for k in range(reach, 0, -1)]
    for (k_even, j_even), (k_odd, j_odd) in zip(ahead, level):
        k_last = k_odd if k_odd == 1 else reach + 2 - k_odd
        k = jnp.where(even, k_even, jnp.where(turn == 3, k_last, k_odd))
        j = jnp.where(even, j_even, j_odd)
        columns = pl.ds(pl.multiple_of(j * piece, piece), piece)

        @pl.when(band + k < bands)
        def _():
            panel_copy(k, j).wait_recv()

            @pl.when((k == 2) | ((k == 3) & (turn == 1)))
            def _():
                relay_copy(k, j).start()

            @pl.when(j == 0)
            def _():
                coef_copy(k).wait_recv()

            mean, scale = coef_in[k - 1, 0:1, columns], coef_in[k - 1, 1:2, columns]

            def rescale(i, _):
                span = pl.ds(pl.multiple_of(i * chunk, chunk), chunk)
                work[span, :] = standard(window[k - 1, span, columns], mean, scale)
                return 0

            lax.fori_loop(0, depth // chunk, rescale, 0)
            correlate(k, j, work)

    for j in range(PIECES):
        finish(0, j)
    for j in range(PIECES):
        for k in range(1, reach + 1):
            @pl.when(band + k < bands)
            def _():
                finish(k, j)

            @pl.when(band + k >= bands)
            def _():
                place = slice(k * width + j * piece, k * width + (j + 1) * piece)
                out_ref[:, place] = jnp.zeros((rows, piece), jnp.float32)
    for k in range(1, reach + 1):
        @pl.when(band >= k)
        def _():
            coef_copy(k).wait_send()

        for j in range(PIECES):
            @pl.when(sends(k))
            def _():
                panel_copy(k, j).wait_send()

            if k > 1:
                @pl.when((band + k < bands) & ((k == 2) | (turn == 1)))
                def _():
                    relay_copy(k, j).wait_send()


def on_device(bands, shards, dosage):
    depth, width = dosage.shape
    reach = (WIN - TILE + width - 1) // width
    rows = width // shards
    f32 = jnp.float32
    dma = pltpu.SemaphoreType.DMA
    return pl.pallas_call(
        functools.partial(kernel, bands, shards, reach, depth * shards),
        out_shape=jax.ShapeDtypeStruct((rows, WIN), f32),
        in_specs=[pl.BlockSpec(memory_space=pltpu.HBM)],
        out_specs=pl.BlockSpec(memory_space=pltpu.VMEM),
        scratch_shapes=[
            pltpu.VMEM((width, depth), jnp.bfloat16),
            pltpu.VMEM((reach + 1, depth, width), jnp.bfloat16),
            pltpu.VMEM((8, width), f32),
            pltpu.VMEM((shards - 1, 8, width), f32),
            pltpu.VMEM((8, width), f32),
            pltpu.VMEM((reach, 8, width), f32),
            pltpu.VMEM((width, WIN), f32),
            pltpu.VMEM((width, WIN), jnp.bfloat16),
            pltpu.VMEM((max(shards // 2 - 1, 1), rows, WIN), f32),
            pltpu.VMEM((shards // 2, rows, WIN), jnp.bfloat16),
            dma((reach, PIECES)), dma((reach, PIECES)),
            dma((shards - 1,)), dma((shards - 1,)),
            dma((reach,)), dma((reach,)),
            dma((reach + 1, PIECES, shards - 1)), dma((reach + 1, PIECES, shards - 1)),
            dma((reach - 1, PIECES)),
            pltpu.VMEM((depth, width // PIECES), jnp.bfloat16),
            pltpu.VMEM((depth, width), jnp.bfloat16),
            dma(()),
        ],
        compiler_params=pltpu.CompilerParams(
            collective_id=0, has_side_effects=True, vmem_limit_bytes=48 * 1024 * 1024
        ),
    )(dosage)


def solution(mesh):
    return jax.shard_map(
        functools.partial(on_device, mesh.shape["band"], mesh.shape["samp"]),
        mesh=mesh,
        in_specs=(P("samp", "band"),),
        out_specs=P(("band", "samp"), None),
        check_vma=False,
    )
```

```python
import functools

import jax
import jax.numpy as jnp
from jax import lax
from jax.experimental import pallas as pl
from jax.experimental.pallas import tpu as pltpu
from jax.sharding import PartitionSpec as P

TILE = 512
WIN = 2048
PIECES = 4
MESH = pl.DeviceIdType.MESH


def remote(src, dst, send, recv, band, samp):
    return pltpu.make_async_remote_copy(
        src_ref=src, dst_ref=dst, send_sem=send, recv_sem=recv,
        device_id=(band, samp), device_id_type=MESH,
    )


def kernel(bands, shards, reach, samples, dosage_ref, out_ref, own_t, window, stats, stats_in, coef,
           coef_in, parts, far_parts, near_in, far_in, panel_s, panel_r, stat_s, stat_r, coef_s, coef_r,
           part_s, part_r, relay_s, work, raw_ref, load_s):
    band = lax.axis_index("band")
    samp = lax.axis_index("samp")
    depth, width = raw_ref.shape
    load = pltpu.make_async_copy(dosage_ref, raw_ref, load_s)
    load.start()
    rows = width // shards
    piece = width // PIECES
    half = shards // 2
    side, seat = samp // half, lax.rem(samp, half)
    near = [side * half + lax.rem(seat + d, half) for d in range(1, half)]
    far = [(1 - side) * half + lax.rem(seat + d, half) for d in range(half)]
    peers = far + near

    barrier = pltpu.get_barrier_semaphore()
    for peer in peers:
        pl.semaphore_signal(barrier, inc=1, device_id=(band, peer), device_id_type=MESH)
    expected = shards - 1
    for k in range(1, reach + 1):
        @pl.when(band >= k)
        def _():
            pl.semaphore_signal(barrier, inc=1, device_id=(band - k, samp), device_id_type=MESH)

        @pl.when(band + k < bands)
        def _():
            pl.semaphore_signal(barrier, inc=1, device_id=(band + k, samp), device_id_type=MESH)
    expected = expected + jnp.minimum(band, reach) + jnp.minimum(bands - 1 - band, reach)
    pl.semaphore_wait(barrier, expected)
    load.wait()

    def panel_copy(k, j):
        columns = pl.ds(pl.multiple_of(j * piece, piece), piece)
        return remote(raw_ref.at[:, columns], window.at[k - 1, :, columns],
                      panel_s.at[k - 1, j], panel_r.at[k - 1, j], jnp.maximum(band - k, 0), samp)

    even = lax.rem(band, 2) == 0
    turn = lax.rem(band, 4)

    def sends(k):
        if k == 1:
            return jnp.logical_not(even)
        if k == 2:
            return (band >= 2) & (turn != 0)
        return even & (band >= 3)

    def relay_copy(k, j):
        columns = pl.ds(pl.multiple_of(j * piece, piece), piece)
        onward = (k == 2) & jnp.logical_not(even)
        target = jnp.clip(jnp.where(onward, band - 1, band + 1), 0, bands - 1)
        slot = jnp.where(k == 3, 1, jnp.where(even, 0, 2))
        return remote(window.at[k - 1, :, columns], window.at[slot, :, columns],
                      relay_s.at[k - 2, j], panel_r.at[slot, j], target, samp)

    def coef_copy(k):
        return remote(coef, coef_in.at[k - 1], coef_s.at[k - 1], coef_r.at[k - 1],
                      jnp.maximum(band - k, 0), samp)

    def part_copy(k, j, d):
        columns = pl.ds(pl.multiple_of(k * width + j * piece, piece), piece)
        source, landing, slot = (far_parts, far_in, d) if d < half else (parts, near_in, d - half)
        return remote(source.at[pl.ds(pl.multiple_of(peers[d] * rows, rows), rows), columns],
                      landing.at[slot, :, columns],
                      part_s.at[k, j, d], part_r.at[k, j, d], band, peers[d])

    def start_panel(k, j):
        @pl.when(sends(k))
        def _():
            panel_copy(k, j).start()

    early = [(k, 0) for k in range(1, reach + 1)]
    later = [(k, j) for j in range(PIECES) for k in range(1, reach + 1) if (k, j) not in early]
    for k, j in early:
        start_panel(k, j)

    step = 64

    def add(i, carry):
        x = raw_ref[pl.ds(pl.multiple_of(i * step, step), step), :].astype(jnp.float32)
        seen = jnp.where(x >= 0.0, 1.0, 0.0)
        value = jnp.where(x >= 0.0, x, 0.0)
        fold = lambda a: jnp.sum(a.reshape(step // 8, 8, width), axis=0)
        return carry[0] + fold(seen), carry[1] + fold(value), carry[2] + fold(value * value)

    zero = jnp.zeros((8, width), jnp.float32)
    sums = lax.fori_loop(0, depth // step, add, (zero, zero, zero))
    stats[...] = jnp.concatenate(
        [jnp.sum(a, axis=0, keepdims=True) for a in sums] + [jnp.zeros((5, width), jnp.float32)], axis=0
    )
    stat_copies = [
        remote(stats, stats_in.at[d], stat_s.at[d], stat_r.at[d], band, peers[d])
        for d in range(shards - 1)
    ]
    for copy in stat_copies:
        copy.start()
    chunk = 256

    def turn_own(i, _):
        span = pl.ds(pl.multiple_of(i * chunk, chunk), chunk)
        own_t[:, span] = raw_ref[span, :].T
        return 0

    lax.fori_loop(0, depth // chunk, turn_own, 0)
    for copy in stat_copies:
        copy.wait()
    sums = stats[...]
    for d in range(shards - 1):
        sums = sums + stats_in[d]
    count, total, square = sums[0:1], sums[1:2], sums[2:3]
    mean = (total + 1.0) / (count + 1.0)
    spread = (square - 2.0 * mean * total + count * mean * mean + 0.5) / (count + 1.0)
    coef[...] = jnp.concatenate(
        [mean, lax.rsqrt(spread), jnp.zeros((6, width), jnp.float32)], axis=0
    )
    for k in range(1, reach + 1):
        @pl.when(band >= k)
        def _():
            coef_copy(k).start()
    for k, j in later:
        start_panel(k, j)

    def standard(x, mean, scale):
        x = x.astype(jnp.float32)
        return jnp.where(x >= 0.0, (x - mean) * scale, 0.0).astype(jnp.bfloat16)

    own = window.at[reach]

    upright = coef[...].T

    def scale_own(i, _):
        span = pl.ds(pl.multiple_of(i * chunk, chunk), chunk)
        own[span, :] = standard(raw_ref[span, :], coef[0:1, :], coef[1:2, :])
        own_t[:, span] = standard(own_t[:, span], upright[:, 0:1], upright[:, 1:2])
        return 0

    lax.fori_loop(0, depth // chunk, scale_own, 0)

    def correlate(k, j, panel):
        place = pl.ds(pl.multiple_of(k * width + j * piece, piece), piece)

        def block(i, _):
            span = pl.ds(pl.multiple_of(i * 256, 256), 256)
            total = jnp.dot(own_t[span, :], panel[...], preferred_element_type=jnp.float32)
            parts[span, place] = total
            far_parts[span, place] = total.astype(jnp.bfloat16)
            return 0

        lax.fori_loop(0, width // 256, block, 0)
        for d in range(shards - 1):
            part_copy(k, j, d).start()
        out_ref[:, place] = parts[pl.ds(pl.multiple_of(samp * rows, rows), rows), place]

    def finish(k, j):
        place = slice(k * width + j * piece, k * width + (j + 1) * piece)
        total = out_ref[:, place]
        for d in range(shards - 1):
            part_copy(k, j, d).wait()
            landed = far_in[d, :, place] if d < half else near_in[d - half, :, place]
            total = total + landed.astype(jnp.float32)
        out_ref[:, place] = total / samples

    for j in range(PIECES):
        correlate(0, j, own.at[:, pl.ds(j * piece, piece)])
    ahead = [(1, 0)]
    for j in range(PIECES):
        ahead += [(1, j + 1)] if j + 1 < PIECES else []
        ahead += [(k, j) for k in range(2, reach + 1)]
    level = [(k, j) for j in range(PIECES) for k in range(reach, 0, -1)]
    for (k_even, j_even), (k_odd, j_odd) in zip(ahead, level):
        k_last = k_odd if k_odd == 1 else reach + 2 - k_odd
        k = jnp.where(even, k_even, jnp.where(turn == 3, k_last, k_odd))
        j = jnp.where(even, j_even, j_odd)
        columns = pl.ds(pl.multiple_of(j * piece, piece), piece)

        @pl.when(band + k < bands)
        def _():
            panel_copy(k, j).wait_recv()

            @pl.when((k == 2) | ((k == 3) & (turn == 1)))
            def _():
                relay_copy(k, j).start()

            @pl.when(j == 0)
            def _():
                coef_copy(k).wait_recv()

            mean, scale = coef_in[k - 1, 0:1, columns], coef_in[k - 1, 1:2, columns]

            def rescale(i, _):
                span = pl.ds(pl.multiple_of(i * chunk, chunk), chunk)
                work[span, :] = standard(window[k - 1, span, columns], mean, scale)
                return 0

            lax.fori_loop(0, depth // chunk, rescale, 0)
            correlate(k, j, work)

    for j in range(PIECES):
        finish(0, j)
    for j in range(PIECES):
        for k in range(1, reach + 1):
            @pl.when(band + k < bands)
            def _():
                finish(k, j)

            @pl.when(band + k >= bands)
            def _():
                place = slice(k * width + j * piece, k * width + (j + 1) * piece)
                out_ref[:, place] = jnp.zeros((rows, piece), jnp.float32)
    for k in range(1, reach + 1):
        @pl.when(band >= k)
        def _():
            coef_copy(k).wait_send()

        for j in range(PIECES):
            @pl.when(sends(k))
            def _():
                panel_copy(k, j).wait_send()

            if k > 1:
                @pl.when((band + k < bands) & ((k == 2) | (turn == 1)))
                def _():
                    relay_copy(k, j).wait_send()


def on_device(bands, shards, dosage):
    depth, width = dosage.shape
    reach = (WIN - TILE + width - 1) // width
    rows = width // shards
    f32 = jnp.float32
    dma = pltpu.SemaphoreType.DMA
    return pl.pallas_call(
        functools.partial(kernel, bands, shards, reach, depth * shards),
        out_shape=jax.ShapeDtypeStruct((rows, WIN), f32),
        in_specs=[pl.BlockSpec(memory_space=pltpu.HBM)],
        out_specs=pl.BlockSpec(memory_space=pltpu.VMEM),
        scratch_shapes=[
            pltpu.VMEM((width, depth), jnp.bfloat16),
            pltpu.VMEM((reach + 1, depth, width), jnp.bfloat16),
            pltpu.VMEM((8, width), f32),
            pltpu.VMEM((shards - 1, 8, width), f32),
            pltpu.VMEM((8, width), f32),
            pltpu.VMEM((reach, 8, width), f32),
            pltpu.VMEM((width, WIN), f32),
            pltpu.VMEM((width, WIN), jnp.bfloat16),
            pltpu.VMEM((max(shards // 2 - 1, 1), rows, WIN), f32),
            pltpu.VMEM((shards // 2, rows, WIN), jnp.bfloat16),
            dma((reach, PIECES)), dma((reach, PIECES)),
            dma((shards - 1,)), dma((shards - 1,)),
            dma((reach,)), dma((reach,)),
            dma((reach + 1, PIECES, shards - 1)), dma((reach + 1, PIECES, shards - 1)),
            dma((reach - 1, PIECES)),
            pltpu.VMEM((depth, width // PIECES), jnp.bfloat16),
            pltpu.VMEM((depth, width), jnp.bfloat16),
            dma(()),
        ],
        compiler_params=pltpu.CompilerParams(
            collective_id=0, has_side_effects=True, vmem_limit_bytes=48 * 1024 * 1024
        ),
    )(dosage)


def solution(mesh):
    return jax.shard_map(
        functools.partial(on_device, mesh.shape["band"], mesh.shape["samp"]),
        mesh=mesh,
        in_specs=(P("samp", "band"),),
        out_specs=P(("band", "samp"), None),
        check_vma=False,
    )
```

```python
import functools

import jax
import jax.numpy as jnp
from jax import lax
from jax.experimental import pallas as pl
from jax.experimental.pallas import tpu as pltpu
from jax.sharding import PartitionSpec as P

TILE = 512
WIN = 2048
PIECES = 4
MESH = pl.DeviceIdType.MESH


def remote(src, dst, send, recv, band, samp):
    return pltpu.make_async_remote_copy(
        src_ref=src, dst_ref=dst, send_sem=send, recv_sem=recv,
        device_id=(band, samp), device_id_type=MESH,
    )


def kernel(bands, shards, reach, samples, dosage_ref, out_ref, own_t, window, stats, stats_in, coef,
           coef_in, parts, far_parts, near_in, far_in, panel_s, panel_r, stat_s, stat_r, coef_s, coef_r,
           part_s, part_r, relay_s, work, raw_ref, load_s):
    band = lax.axis_index("band")
    samp = lax.axis_index("samp")
    depth, width = raw_ref.shape
    load = pltpu.make_async_copy(dosage_ref, raw_ref, load_s)
    load.start()
    rows = width // shards
    piece = width // PIECES
    half = shards // 2
    side, seat = samp // half, lax.rem(samp, half)
    near = [side * half + lax.rem(seat + d, half) for d in range(1, half)]
    far = [(1 - side) * half + lax.rem(seat + d, half) for d in range(half)]
    peers = far + near

    barrier = pltpu.get_barrier_semaphore()
    for peer in peers:
        pl.semaphore_signal(barrier, inc=1, device_id=(band, peer), device_id_type=MESH)
    expected = shards - 1
    for k in range(1, reach + 1):
        @pl.when(band >= k)
        def _():
            pl.semaphore_signal(barrier, inc=1, device_id=(band - k, samp), device_id_type=MESH)

        @pl.when(band + k < bands)
        def _():
            pl.semaphore_signal(barrier, inc=1, device_id=(band + k, samp), device_id_type=MESH)
    expected = expected + jnp.minimum(band, reach) + jnp.minimum(bands - 1 - band, reach)
    pl.semaphore_wait(barrier, expected)
    load.wait()

    def panel_copy(k, j):
        columns = pl.ds(pl.multiple_of(j * piece, piece), piece)
        return remote(raw_ref.at[:, columns], window.at[k - 1, :, columns],
                      panel_s.at[k - 1, j], panel_r.at[k - 1, j], jnp.maximum(band - k, 0), samp)

    even = lax.rem(band, 2) == 0
    turn = lax.rem(band, 4)

    def sends(k):
        if k == 1:
            return jnp.logical_not(even)
        if k == 2:
            return (band >= 2) & (turn != 0)
        return even & (band >= 3)

    def relay_copy(k, j):
        columns = pl.ds(pl.multiple_of(j * piece, piece), piece)
        onward = (k == 2) & jnp.logical_not(even)
        target = jnp.clip(jnp.where(onward, band - 1, band + 1), 0, bands - 1)
        slot = jnp.where(k == 3, 1, jnp.where(even, 0, 2))
        return remote(window.at[k - 1, :, columns], window.at[slot, :, columns],
                      relay_s.at[k - 2, j], panel_r.at[slot, j], target, samp)

    def coef_copy(k):
        return remote(coef, coef_in.at[k - 1], coef_s.at[k - 1], coef_r.at[k - 1],
                      jnp.maximum(band - k, 0), samp)

    def part_copy(k, j, d):
        columns = pl.ds(pl.multiple_of(k * width + j * piece, piece), piece)
        source, landing, slot = (far_parts, far_in, d) if d < half else (parts, near_in, d - half)
        return remote(source.at[pl.ds(pl.multiple_of(peers[d] * rows, rows), rows), columns],
                      landing.at[slot, :, columns],
                      part_s.at[k, j, d], part_r.at[k, j, d], band, peers[d])

    def start_panel(k, j):
        @pl.when(sends(k))
        def _():
            panel_copy(k, j).start()

    early = [(k, 0) for k in range(1, reach + 1)]
    later = [(k, j) for j in range(PIECES) for k in range(1, reach + 1) if (k, j) not in early]
    for k, j in early:
        start_panel(k, j)

    step = 64

    def add(i, carry):
        x = raw_ref[pl.ds(pl.multiple_of(i * step, step), step), :].astype(jnp.float32)
        seen = jnp.where(x >= 0.0, 1.0, 0.0)
        value = jnp.where(x >= 0.0, x, 0.0)
        fold = lambda a: jnp.sum(a.reshape(step // 8, 8, width), axis=0)
        return carry[0] + fold(seen), carry[1] + fold(value), carry[2] + fold(value * value)

    zero = jnp.zeros((8, width), jnp.float32)
    sums = lax.fori_loop(0, depth // step, add, (zero, zero, zero))
    stats[...] = jnp.concatenate(
        [jnp.sum(a, axis=0, keepdims=True) for a in sums] + [jnp.zeros((5, width), jnp.float32)], axis=0
    )
    stat_copies = [
        remote(stats, stats_in.at[d], stat_s.at[d], stat_r.at[d], band, peers[d])
        for d in range(shards - 1)
    ]
    for copy in stat_copies:
        copy.start()
    for copy in stat_copies:
        copy.wait()
    sums = stats[...]
    for d in range(shards - 1):
        sums = sums + stats_in[d]
    count, total, square = sums[0:1], sums[1:2], sums[2:3]
    mean = (total + 1.0) / (count + 1.0)
    spread = (square - 2.0 * mean * total + count * mean * mean + 0.5) / (count + 1.0)
    coef[...] = jnp.concatenate(
        [mean, lax.rsqrt(spread), jnp.zeros((6, width), jnp.float32)], axis=0
    )
    for k in range(1, reach + 1):
        @pl.when(band >= k)
        def _():
            coef_copy(k).start()
    for k, j in later:
        start_panel(k, j)

    chunk = 256

    def standard(x, mean, scale):
        x = x.astype(jnp.float32)
        return jnp.where(x >= 0.0, (x - mean) * scale, 0.0).astype(jnp.bfloat16)

    own = window.at[reach]

    def scale_own(i, _):
        span = pl.ds(pl.multiple_of(i * chunk, chunk), chunk)
        scaled = standard(raw_ref[span, :], coef[0:1, :], coef[1:2, :])
        own[span, :] = scaled
        own_t[:, span] = scaled.T
        return 0

    lax.fori_loop(0, depth // chunk, scale_own, 0)

    def correlate(k, j, panel):
        place = pl.ds(pl.multiple_of(k * width + j * piece, piece), piece)

        def block(i, _):
            span = pl.ds(pl.multiple_of(i * 256, 256), 256)
            total = jnp.dot(own_t[span, :], panel[...], preferred_element_type=jnp.float32)
            parts[span, place] = total
            far_parts[span, place] = total.astype(jnp.bfloat16)
            return 0

        lax.fori_loop(0, width // 256, block, 0)
        for d in range(shards - 1):
            part_copy(k, j, d).start()
        out_ref[:, place] = parts[pl.ds(pl.multiple_of(samp * rows, rows), rows), place]

    def finish(k, j):
        place = slice(k * width + j * piece, k * width + (j + 1) * piece)
        total = out_ref[:, place]
        for d in range(shards - 1):
            part_copy(k, j, d).wait()
            landed = far_in[d, :, place] if d < half else near_in[d - half, :, place]
            total = total + landed.astype(jnp.float32)
        out_ref[:, place] = total / samples

    for j in range(PIECES):
        correlate(0, j, own.at[:, pl.ds(j * piece, piece)])
    ahead = [(1, 0)]
    for j in range(PIECES):
        ahead += [(1, j + 1)] if j + 1 < PIECES else []
        ahead += [(k, j) for k in range(2, reach + 1)]
    level = [(k, j) for j in range(PIECES) for k in range(reach, 0, -1)]
    for place, ((k_even, j_even), (k_odd, j_odd)) in enumerate(zip(ahead, level)):
        if place == len(level) - reach:
            for j in range(PIECES):
                finish(0, j)
        k_last = k_odd if k_odd == 1 else reach + 2 - k_odd
        k = jnp.where(even, k_even, jnp.where(turn == 3, k_last, k_odd))
        j = jnp.where(even, j_even, j_odd)
        columns = pl.ds(pl.multiple_of(j * piece, piece), piece)

        @pl.when(band + k < bands)
        def _():
            panel_copy(k, j).wait_recv()

            @pl.when((k == 2) | ((k == 3) & (turn == 1)))
            def _():
                relay_copy(k, j).start()

            @pl.when(j == 0)
            def _():
                coef_copy(k).wait_recv()

            mean, scale = coef_in[k - 1, 0:1, columns], coef_in[k - 1, 1:2, columns]

            def rescale(i, _):
                span = pl.ds(pl.multiple_of(i * chunk, chunk), chunk)
                work[span, :] = standard(window[k - 1, span, columns], mean, scale)
                return 0

            lax.fori_loop(0, depth // chunk, rescale, 0)
            correlate(k, j, work)

    for j in range(PIECES):
        for k in range(1, reach + 1):
            @pl.when(band + k < bands)
            def _():
                finish(k, j)

            @pl.when(band + k >= bands)
            def _():
                place = slice(k * width + j * piece, k * width + (j + 1) * piece)
                out_ref[:, place] = jnp.zeros((rows, piece), jnp.float32)
    for k in range(1, reach + 1):
        @pl.when(band >= k)
        def _():
            coef_copy(k).wait_send()

        for j in range(PIECES):
            @pl.when(sends(k))
            def _():
                panel_copy(k, j).wait_send()

            if k > 1:
                @pl.when((band + k < bands) & ((k == 2) | (turn == 1)))
                def _():
                    relay_copy(k, j).wait_send()


def on_device(bands, shards, dosage):
    depth, width = dosage.shape
    reach = (WIN - TILE + width - 1) // width
    rows = width // shards
    f32 = jnp.float32
    dma = pltpu.SemaphoreType.DMA
    return pl.pallas_call(
        functools.partial(kernel, bands, shards, reach, depth * shards),
        out_shape=jax.ShapeDtypeStruct((rows, WIN), f32),
        in_specs=[pl.BlockSpec(memory_space=pltpu.HBM)],
        out_specs=pl.BlockSpec(memory_space=pltpu.VMEM),
        scratch_shapes=[
            pltpu.VMEM((width, depth), jnp.bfloat16),
            pltpu.VMEM((reach + 1, depth, width), jnp.bfloat16),
            pltpu.VMEM((8, width), f32),
            pltpu.VMEM((shards - 1, 8, width), f32),
            pltpu.VMEM((8, width), f32),
            pltpu.VMEM((reach, 8, width), f32),
            pltpu.VMEM((width, WIN), f32),
            pltpu.VMEM((width, WIN), jnp.bfloat16),
            pltpu.VMEM((max(shards // 2 - 1, 1), rows, WIN), f32),
            pltpu.VMEM((shards // 2, rows, WIN), jnp.bfloat16),
            dma((reach, PIECES)), dma((reach, PIECES)),
            dma((shards - 1,)), dma((shards - 1,)),
            dma((reach,)), dma((reach,)),
            dma((reach + 1, PIECES, shards - 1)), dma((reach + 1, PIECES, shards - 1)),
            dma((reach - 1, PIECES)),
            pltpu.VMEM((depth, width // PIECES), jnp.bfloat16),
            pltpu.VMEM((depth, width), jnp.bfloat16),
            dma(()),
        ],
        compiler_params=pltpu.CompilerParams(
            collective_id=0, has_side_effects=True, vmem_limit_bytes=48 * 1024 * 1024
        ),
    )(dosage)


def solution(mesh):
    return jax.shard_map(
        functools.partial(on_device, mesh.shape["band"], mesh.shape["samp"]),
        mesh=mesh,
        in_specs=(P("samp", "band"),),
        out_specs=P(("band", "samp"), None),
        check_vma=False,
    )
```
